32 devices in a mesh: section: 2 (over core), fsdp: 16 (over z, y, x).
Axes of the slice: x: 2, y: 2, z: 4, core: 2. Of those that a mesh axis runs over, the one named last changes fastest.
Arguments:
- tokens: bfloat16 [2, 2048, 2048], P(None, 'fsdp'), may hold values from -6 to 6
- norm_gains: float32 [2, 2048], P('section'), may hold values from 0.5 to 1.5
- router_cols: bfloat16 [2, 2048, 1], P('section'), may hold values from -0.125 to 0.125
- gate_weight: bfloat16 [2, 1, 1024, 2048], P('section', None, 'fsdp'), may hold values from -0.125 to 0.125
- up_weight: bfloat16 [2, 1, 1024, 2048], P('section', None, 'fsdp'), may hold values from -0.125 to 0.125
- down_weight: bfloat16 [2, 1, 1024, 2048], P('section', None, 'fsdp'), may hold values from -0.25 to 0.25
- expert_ids: int32 [2, 2, 2048, 8], P('section', None, 'fsdp'), may hold values from 0 to 63, all different within a row; in each aligned block of 128 rows (0 to 127, 128 to 255, ..., all dimensions but the last counted through in order) at most 32 rows name the same one
Outputs:
- layer_states: bfloat16 [2, 2, 2048, 2048], P('section', None, 'fsdp')
The draws below stay inside these ranges and needn't reach their ends.
Inputs may be any that keep to these rules, and one draw needn't show every extreme that they name: `expert_ids`: within one layer and micro-batch, no expert is named by more than 32 of the 128 tokens of one fsdp index; a token names 8 different experts.
All inputs are finite; a program needn't handle non-finite values.
Results may differ from the reference program's by a relative error of at most 0.0013.
Values may be sent and summed in bfloat16 or wider, within the bound.
A program may use at most 128 MiB of HBM per device.

```python
import math
import jax
import jax.numpy as jnp
import numpy as np
from jax import lax

D = 2048
FF = 1024
EXPERTS = 64
TOP = 8
FLY = 1
MB = 2
TOK_DEV = 128
MOST = 32
LAYERS = 2
TOKENS = 2048


def strengthened(drawn, own_key, source, target, shards_of, factor):
    def block_of(axis_at):
        return (jnp.arange(drawn.shape[axis_at]) // (drawn.shape[axis_at] // shards_of)).reshape((-1,) + (1,) * (drawn.ndim - 1 - axis_at))

    one_side = jax.random.permutation(own_key, shards_of)[block_of(target)]
    second = (block_of(target) + shards_of // 2) % shards_of
    return jnp.where((block_of(source) == one_side) | (block_of(source) == second), factor * drawn, drawn)


def level_of(rng, shape, shards, least, top_value):
    def one(position, shards_of):
        draws = jax.random.uniform(jax.random.fold_in(jax.random.fold_in(rng, 6), position), (shards_of,), jnp.float32, least / len(shards), top_value / len(shards))
        return jnp.repeat(jnp.exp(draws), shape[position] // shards_of).reshape((-1,) + (1,) * (len(shape) - position - 1))

    loudness = one(*shards[0])
    for cut in shards[1:]:
        loudness = loudness * one(*cut)
    return loudness


def deal_out(key, own, number, rows, number_of, top, reach, skew):
    order = jax.random.permutation(key, number_of)
    heavy_load, usual = shares(number_of, rows * top, reach, skew, True), shares(number_of, rows * top, reach, skew, False)
    places = jnp.arange(number_of)

    def named(tallies, offset_by):
        used = int((tallies > 0).sum())
        fixed = max(1, used // 4)
        shifted = fixed + (places - fixed + offset_by * (used - fixed)) % max(1, number_of - fixed)
        return jnp.zeros((number_of,), jnp.int32).at[order[jnp.where(places < fixed, places, shifted)]].set(jnp.asarray(tallies, jnp.int32))

    tallies = jnp.where(number % 4 == 0, named(heavy_load, number // 4), named(usual, number - number // 4 - 1))
    mixed = jax.random.permutation(jax.random.fold_in(own, 3), number_of)
    giver, taker = mixed[0:number_of // 2 * 2:2], mixed[1:number_of // 2 * 2:2]
    margin = jnp.minimum(tallies[giver] - 1, reach - tallies[taker]) // 2
    margin = jnp.where((giver == order[0]) | (taker == order[0]) | (tallies[taker] == 0), 0, jnp.maximum(margin, 0))
    shifted = jax.random.randint(jax.random.fold_in(own, 4), (number_of // 2,), 0, 1 << 20) % (margin + 1)
    tallies = tallies.at[giver].add(-shifted).at[taker].add(shifted)
    labels = jnp.searchsorted(jnp.cumsum(tallies), jnp.arange(rows * top), side="right").astype(jnp.int32)
    grid = labels.reshape(top, rows).T
    grid = grid[jax.random.permutation(jax.random.fold_in(own, 1), rows)]
    offset_by = jax.random.randint(jax.random.fold_in(own, 2), (rows, 1), 0, top)
    return jnp.take_along_axis(grid, (jnp.arange(top)[None, :] + offset_by) % top, axis=1)


def shares(count, total, bound, lean, full):
    portions = [(1 << 20) // math.isqrt(grade ** lean) + 1 for grade in range(1, count + 1)]
    largest = bound if full else min(bound, max(-(-total // count), total * portions[0] // sum(portions)))
    least = 1 if total - largest >= count - 1 else 0
    counts, spare = [largest] + [least] * (count - 1), total - largest - least * (count - 1)
    while spare > 0:
        free = [i for i in range(1, count) if counts[i] < largest] or [i for i in range(1, count) if counts[i] < bound]
        whole, budget = sum([portions[i] for i in free]), spare
        for i in free:
            addition = min(bound - counts[i], max(1, budget * portions[i] // whole), spare)
            counts[i] = counts[i] + addition
            spare = spare - addition
    return np.array(counts)


def gaussian(rng, dims, width, limit, split=(), held_as=jnp.bfloat16):
    entries = width * jax.random.normal(rng, dims, jnp.float32)
    if split:
        entries = entries * level_of(rng, dims, split, -0.22, 0.18)
    return jnp.clip(entries, -limit, limit).astype(held_as)


def bell_draw_with(own_key, extent, width, limit, split, heavy, kind=jnp.bfloat16):
    values = width * jax.random.normal(own_key, extent, jnp.float32)
    if split:
        values = values * level_of(own_key, extent, split, -0.22, 0.18)
    return jnp.clip(strengthened(values, jax.random.fold_in(own_key, 3), *heavy), -limit, limit).astype(kind)


def setup_inputs(seed: int = 0) -> dict:
    splits = jax.random.split(jax.random.key(seed), 8)
    tokens = gaussian(splits[0], (MB, TOKENS, D), 1.0, 6.0, ((1, 16),))
    norm_gains = jnp.clip(1.0 + 0.1 * jax.random.normal(splits[1], (LAYERS, D), jnp.float32), 0.5, 1.5)
    router_cols = gaussian(splits[2], (LAYERS, D, FLY), D ** -0.5, 0.125, ((0, 2),))
    gate_weight = gaussian(splits[3], (LAYERS, FLY, FF, D), D ** -0.5, 0.125, ((0, 2), (2, 16)))
    up_weight = gaussian(splits[4], (LAYERS, FLY, FF, D), D ** -0.5, 0.125, ((0, 2), (2, 16)))
    down_weight = bell_draw_with(splits[5], (LAYERS, FLY, FF, D), FF ** -0.5, 0.25, ((0, 2), (2, 16)), (2, 3, 16, 2.0))
    expert_ids_keys = jax.random.split(jax.random.fold_in(splits[6], 1), LAYERS * MB * TOKENS // TOK_DEV)
    expert_ids_turns = jax.random.permutation(jax.random.fold_in(splits[6], 3), LAYERS * MB * TOKENS // TOK_DEV)
    expert_ids = jax.vmap(lambda own, number: deal_out(jax.random.fold_in(splits[6], 2), own, number, TOK_DEV, EXPERTS, TOP, MOST, 2))(expert_ids_keys, expert_ids_turns).reshape((LAYERS, MB, TOKENS, TOP))
    return {"tokens": tokens, "norm_gains": norm_gains, "router_cols": router_cols, "gate_weight": gate_weight, "up_weight": up_weight, "down_weight": down_weight, "expert_ids": expert_ids}


def normalize(hidden, gain):
    widened = hidden.astype(jnp.float32)
    mean_square = lax.optimization_barrier(jnp.mean(widened * widened, axis=-1, keepdims=True))
    normed = (widened * lax.rsqrt(mean_square + 1e-05) * gain).astype(jnp.bfloat16)
    return (widened, normed)

def swiglu(token_rows, gate_rows, up_rows, down_rows):
    contract_dims = (((1,), (1,)), ((), ()))
    gate_proj = lax.dot_general(token_rows, gate_rows, contract_dims, preferred_element_type=jnp.float32)
    up_proj = lax.dot_general(token_rows, up_rows, contract_dims, preferred_element_type=jnp.float32)
    activated = (jax.nn.silu(gate_proj) * up_proj).astype(jnp.bfloat16)
    return jnp.dot(activated, down_rows, preferred_element_type=jnp.float32)

def reference(tokens, norm_gains, router_cols, gate_weight, up_weight, down_weight, expert_ids):
    current = tokens
    stacked_layers = []
    for layer_index in range(LAYERS):
        micro_outs = []
        for micro_index in range(MB):
            widened, normed = normalize(current[micro_index], norm_gains[layer_index])
            scores = jax.nn.sigmoid(jnp.dot(normed, router_cols[layer_index], preferred_element_type=jnp.float32))
            update = jnp.zeros(widened.shape, jnp.float32)
            for expert_slot in range(FLY):
                chosen = jnp.any(expert_ids[layer_index, micro_index] == expert_slot, axis=-1)
                weight = jnp.where(chosen, scores[:, expert_slot], jnp.zeros_like(scores[:, expert_slot]))
                expert_out = swiglu(normed, gate_weight[layer_index, expert_slot], up_weight[layer_index, expert_slot], down_weight[layer_index, expert_slot])
                update = update + weight[:, None] * expert_out
            micro_outs.append((widened + update).astype(jnp.bfloat16))
        current = jnp.stack(micro_outs)
        stacked_layers.append(current)
    return jnp.stack(stacked_layers)
```

```python
import functools

import jax
import jax.numpy as jnp
from jax import lax
from jax.experimental import pallas as pl
from jax.experimental.pallas import tpu as pltpu
from jax.sharding import PartitionSpec as P

MESH = pl.DeviceIdType.MESH
BF16_ROWS = 16
PEERS = 4
AHEAD = 4
FIRST = 0
EPS = 1e-05


def silu(v):
    return v / (1.0 + jnp.exp(-v))


def across(lhs, rhs):
    return lax.dot_general(lhs, rhs, (((1,), (1,)), ((), ())), preferred_element_type=jnp.float32)


def plain(lhs, rhs):
    return jnp.dot(lhs, rhs, preferred_element_type=jnp.float32)


def kernel(
    n, most,
    tokens, gain, router, gate, up, down, ids,
    out,
    base, held, hnext, early, weights, picked, picked_in, gain_in, outc, outc_in, xbuf, xnext, pbuf, psend, mine, across_part,
    w_send, w_recv, x_send, x_recv, p_send, p_recv, o_send, o_recv, l_sem, go,
):
    sec = lax.axis_index("section")
    me = lax.axis_index("fsdp")
    micros, rows, width = tokens.shape
    hid = gate.shape[0]
    half = hid // 2
    group_rows = PEERS * most
    other = 1 - sec

    by_x = 1 - 2 * lax.rem(me, 2)
    by_y = 2 - 4 * lax.rem(lax.div(me, 2), 2)
    by_z = 4 - 8 * lax.rem(lax.div(me, 4), 2)
    by_far = 8 - 16 * lax.rem(lax.div(me, 8), 2)
    near = [me, me + by_z, me + by_far, me + by_z + by_far]
    cross = [me, me + by_y, me + by_z, me + by_y + by_z]
    peer = [a + sec * (b - a) for a, b in zip(near, cross)]
    at_x = me + by_x
    at_y = me + by_y
    far = me + by_far

    barrier = pltpu.get_barrier_semaphore()
    met = [(sec, p) for p in [at_x, at_y, me + by_z, far, me + by_z + by_far, me + by_y + by_z]] + [(other, p) for p in cross]
    for device in met:
        pl.semaphore_signal(barrier, inc=1, device_id=device, device_id_type=MESH)

    own = (gate, up, down)
    chunks = [(a, h) for a in range(3) for h in range(2)]

    fetch = [pltpu.make_async_copy(tokens, base, l_sem.at[3])]
    fetch += [pltpu.make_async_copy(own[a], weights.at[a, pl.ds(0, hid)], l_sem.at[a]) for a in range(3)]
    for copy in fetch:
        copy.start()

    def weight_copy(slot, chunk, target, source_slot=None):
        a, h = chunks[chunk]
        span = pl.ds(h * half, half)
        if source_slot is None:
            src = own[a].at[span]
        else:
            src = weights.at[a, pl.ds(source_slot * hid + h * half, half)]
        return pltpu.make_async_remote_copy(
            src_ref=src,
            dst_ref=weights.at[a, pl.ds(slot * hid + h * half, half)],
            send_sem=w_send.at[slot, chunk],
            recv_sem=w_recv.at[slot, chunk],
            device_id=(sec, target),
            device_id_type=MESH,
        )

    def x_copy(chunk):
        return weight_copy(1, chunk, at_x)

    def y_copy(chunk):
        return weight_copy(2, chunk, at_y)

    def far_copy(chunk):
        return weight_copy(2, chunk, far)

    def turn_copy(chunk):
        if chunk % 2 == 0:
            return weight_copy(3, chunk, at_x, 2)
        return weight_copy(3, chunk, at_y, 1)

    def far_turn_copy(chunk):
        return weight_copy(3, chunk, at_x, 2)

    def block(m, j):
        return pl.ds((m * PEERS + j) * most, most)

    def share_of(m):
        return pl.ds(m * most, most)

    def token_copy(m, j):
        return pltpu.make_async_remote_copy(
            src_ref=xbuf.at[block(m, 0)], dst_ref=xbuf.at[block(m, j)],
            send_sem=x_send.at[m, j], recv_sem=x_recv.at[m, j],
            device_id=(sec, peer[j]), device_id_type=MESH,
        )

    def token_relay(m):
        return pltpu.make_async_remote_copy(
            src_ref=xbuf.at[block(m, PEERS - 2)], dst_ref=xbuf.at[block(m, PEERS - 1)],
            send_sem=x_send.at[m, PEERS - 1], recv_sem=x_recv.at[m, PEERS - 1],
            device_id=(sec, peer[1]), device_id_type=MESH,
        )

    def onward_copy(m, j):
        return pltpu.make_async_remote_copy(
            src_ref=xnext.at[share_of(m)], dst_ref=xbuf.at[block(m, j)],
            send_sem=x_send.at[micros + m, j], recv_sem=x_recv.at[m, j],
            device_id=(other, cross[j]), device_id_type=MESH,
        )

    def partial_copy(m, j):
        return pltpu.make_async_remote_copy(
            src_ref=psend.at[block(m, j)], dst_ref=pbuf.at[block(m, j)],
            send_sem=p_send.at[m, j], recv_sem=p_recv.at[m, j],
            device_id=(sec, peer[j]), device_id_type=MESH,
        )

    def early_copy(m):
        return pltpu.make_async_remote_copy(
            src_ref=psend.at[block(m, PEERS - 1)], dst_ref=pbuf.at[block(m, PEERS - 1)],
            send_sem=p_send.at[m, PEERS - 1], recv_sem=p_recv.at[m, PEERS - 1],
            device_id=(sec, peer[1]), device_id_type=MESH,
        )

    def pass_copy(src, dst, k):
        return pltpu.make_async_remote_copy(
            src_ref=src, dst_ref=dst, send_sem=o_send.at[k], recv_sem=o_recv.at[k],
            device_id=(other, me), device_id_type=MESH,
        )

    pick_copy = pass_copy(picked, picked_in, 0)
    gain_copy = pass_copy(gain, gain_in, 1)
    held_copy = pass_copy(hnext, held, 2)
    outc_copy = pass_copy(outc, outc_in, 3)

    def norm(compact, scale):
        mean_square = jnp.mean(compact * compact, axis=-1, keepdims=True)
        return (compact * lax.rsqrt(mean_square + EPS) * scale).astype(jnp.bfloat16)

    def turned(picks):
        return jnp.transpose(picks.astype(jnp.float32))[0:most].astype(jnp.bfloat16)

    def merge(m, picks, compact, under):
        placed = plain(picks[m][:, 0:most], compact[m * most:(m + 1) * most, :])
        chosen = jnp.sum(picks[m].astype(jnp.float32), axis=1, keepdims=True) > 0.5
        return jnp.where(chosen, placed, under.astype(jnp.float32)).astype(jnp.bfloat16)

    with jax.named_scope("pick"):
        at_row = lax.broadcasted_iota(jnp.int32, (rows, rows), 0)
        at_col = lax.broadcasted_iota(jnp.int32, (rows, rows), 1)
        lower = jnp.where(at_row >= at_col, 1.0, 0.0).astype(jnp.bfloat16)
        for m in range(micros):
            named = jnp.sum(jnp.where(ids[m] == 0, 1.0, 0.0), axis=0, keepdims=True)
            spread = jnp.transpose(jnp.broadcast_to(named, (rows, rows)))
            rank = plain(lower, spread.astype(jnp.bfloat16))
            hit = (rank.astype(jnp.int32) - 1 == at_col) & (spread > 0.5)
            picked[m] = jnp.where(hit, 1.0, 0.0).astype(jnp.bfloat16)
        for copy in fetch:
            copy.wait()

    @pl.when(sec == 0)
    def _():
        for m in range(micros):
            compact = plain(turned(picked[m]), base[m])
            held[share_of(m), :] = compact.astype(jnp.bfloat16)
            xbuf[block(m, 0), :] = norm(compact, gain[...])

    with jax.named_scope("bar"):
        pl.semaphore_wait(barrier, len(met))

    @pl.when(sec == 0)
    def _():
        for m in range(micros):
            for j in range(PEERS - 2, 0, -1):
                token_copy(m, j).start()
        for c in range(len(chunks)):
            x_copy(c).start()
            y_copy(c).start()
        pick_copy.start()
        pick_copy.wait_recv()
        gain_copy.wait_recv()
        for m in range(micros):
            token_copy(m, PEERS - 2).wait_send()
        pl.semaphore_signal(go.at[0], inc=1, device_id=(other, me), device_id_type=MESH)
        for m in range(micros):
            early[share_of(m), :] = plain(turned(picked_in[m]), base[m])

        with jax.named_scope("xrelay"):
            for m in range(micros):
                token_copy(m, PEERS - 2).wait_recv()
                token_relay(m).start()
        for c in range(len(chunks)):
            with jax.named_scope("wrelay"):
                (y_copy if c % 2 == 0 else x_copy)(c).wait_recv()
            turn_copy(c).start()

    @pl.when(sec == 1)
    def _():
        for c in range(FIRST):
            far_copy(c).start()
        gain_copy.start()
        pick_copy.start()
        pick_copy.wait_recv()
        with jax.named_scope("go0"):
            pl.semaphore_wait(go.at[0], 1)
        for c in range(FIRST, AHEAD):
            far_copy(c).start()
        with jax.named_scope("go1"):
            pl.semaphore_wait(go.at[1], 1)
        for c in range(AHEAD):
            x_copy(c).start()
            with jax.named_scope("frelay"):
                far_copy(c).wait_recv()
            far_turn_copy(c).start()
        for c in range(AHEAD, len(chunks)):
            x_copy(c).start()
        with jax.named_scope("go2"):
            pl.semaphore_wait(go.at[2], 1)
        for c in range(AHEAD, len(chunks)):
            far_copy(c).start()
        for c in range(AHEAD, len(chunks)):
            with jax.named_scope("frelay"):
                far_copy(c).wait_recv()
            far_turn_copy(c).start()

    def wait_weights(some):
        for c in some:
            @pl.when(sec == 0)
            def _():
                (x_copy if c % 2 == 0 else y_copy)(c).wait_recv()
                turn_copy(c).wait_recv()

            @pl.when(sec == 1)
            def _():
                x_copy(c).wait_recv()
                far_turn_copy(c).wait_recv()

    with jax.named_scope("ww"):
        wait_weights(range(4))

    @pl.when(sec == 0)
    def _():
        with jax.named_scope("wtok"):
            for m in range(micros):
                token_copy(m, 1).wait_recv()
                token_relay(m).wait_recv()

    for m in range(micros):
        @pl.when(sec == 1)
        def _():
            with jax.named_scope("won"):
                for j in range(PEERS):
                    onward_copy(m, j).wait_recv()

        with jax.named_scope("gu"):
            x = xbuf[pl.ds(m * group_rows, group_rows), :]
            activated = (silu(across(x, weights[0])) * across(x, weights[1])).astype(jnp.bfloat16)
        if m == 0:
            with jax.named_scope("ww2"):
                wait_weights(range(4, len(chunks)))

            @pl.when(sec == 0)
            def _():
                pl.semaphore_signal(go.at[1], inc=1, device_id=(other, me), device_id_type=MESH)

        with jax.named_scope("down"):
            partial = plain(activated, weights[2])
            mine[share_of(m), :] = partial[0:most]
            psend[pl.ds(m * group_rows, group_rows), :] = partial.astype(jnp.bfloat16)
        @pl.when(sec == 0)
        def _():
            across_part[share_of(m), :] = partial[2 * most:3 * most]
            early_copy(m).start()
            if m == micros - 1:
                for k in range(micros):
                    partial_copy(k, 1).start()

        @pl.when(sec == 1)
        def _():
            for j in range(PEERS - 1, 0, -1):
                partial_copy(m, j).start()

    @pl.when(sec == 0)
    def _():
        for m in range(micros):
            with jax.named_scope("wearly"):
                early_copy(m).wait_recv()
            joined = across_part[share_of(m), :] + pbuf[block(m, PEERS - 1), :].astype(jnp.float32)
            psend[block(m, 2), :] = joined.astype(jnp.bfloat16)
            partial_copy(m, 2).start()
        for m in range(micros):
            with jax.named_scope("wsent"):
                partial_copy(m, 2).wait_send()
        pl.semaphore_signal(go.at[2], inc=1, device_id=(other, me), device_id_type=MESH)

    @pl.when(sec == 1)
    def _():
        held_copy.wait_recv()
        outc_copy.wait_recv()
        for m in range(micros):
            base[m] = merge(m, picked_in, outc_in, base[m])

    for m in range(micros):
        span = share_of(m)
        with jax.named_scope("wpart"):
            score = jnp.sum(xbuf[block(m, 0), :].astype(jnp.float32) * router[...].astype(jnp.float32), axis=1, keepdims=True)
            share = 1.0 / (1.0 + jnp.exp(-score))
            for j in range(1, PEERS - 1):
                partial_copy(m, j).wait_recv()
            last = partial_copy(m, PEERS - 1)
            pl.when(sec == 1)(last.wait_recv)
            update = mine[span, :]
            for j in range(1, PEERS - 1):
                update = update + pbuf[block(m, j), :].astype(jnp.float32)
            over = pbuf[block(m, PEERS - 1), :].astype(jnp.float32)
            update = update + jnp.where(sec == 1, over, 0.0)
        outc[span, :] = (held[span, :].astype(jnp.float32) + share * update).astype(jnp.bfloat16)

        @pl.when(sec == 0)
        def _():
            with jax.named_scope("next"):
                again = plain(turned(picked_in[m]), picked[m][:, 0:most])
                changed = jnp.sum(again, axis=1, keepdims=True) > 0.5
                following = jnp.where(changed, plain(again.astype(jnp.bfloat16), outc[span, :]), early[span, :])
                xnext[span, :] = norm(following, gain_in[...])
                hnext[span, :] = following.astype(jnp.bfloat16)
            for j in range(PEERS - 1, -1, -1):
                onward_copy(m, j).start()

        @pl.when(sec == 1)
        def _():
            out[m] = merge(m, picked, outc, base[m])

    @pl.when(sec == 0)
    def _():
        held_copy.start()
        outc_copy.start()
        for m in range(micros):
            out[m] = merge(m, picked, outc, base[m])

    for c in range(len(chunks)):
        x_copy(c).wait_send()

        @pl.when(sec == 0)
        def _():
            y_copy(c).wait_send()
            turn_copy(c).wait_send()

        @pl.when(sec == 1)
        def _():
            far_copy(c).wait_send()
            far_turn_copy(c).wait_send()
    pick_copy.wait_send()
    for m in range(micros):
        partial_copy(m, 1).wait_send()

        @pl.when(sec == 0)
        def _():
            early_copy(m).wait_send()

        @pl.when(sec == 1)
        def _():
            partial_copy(m, 2).wait_send()
            partial_copy(m, PEERS - 1).wait_send()

    @pl.when(sec == 0)
    def _():
        held_copy.wait_send()
        outc_copy.wait_send()
        for m in range(micros):
            token_copy(m, 1).wait_send()
            token_relay(m).wait_send()
            for j in range(PEERS):
                onward_copy(m, j).wait_send()

    @pl.when(sec == 1)
    def _():
        gain_copy.wait_send()


def grouped(n, tokens, norm_gains, router_cols, gate_weight, up_weight, down_weight, expert_ids):
    micros, rows, width = tokens.shape
    hid = gate_weight.shape[2]
    most = rows // 4
    slots = n // PEERS
    own_rows = micros * most
    all_rows = PEERS * own_rows
    dma = pltpu.SemaphoreType.DMA
    vmem = pl.BlockSpec(memory_space=pltpu.VMEM)
    whole = pl.BlockSpec(memory_space=pltpu.HBM)
    half = lambda *shape: pltpu.VMEM(shape, jnp.bfloat16)
    full = lambda *shape: pltpu.VMEM(shape, jnp.float32)
    result = pl.pallas_call(
        functools.partial(kernel, n, most),
        out_shape=jax.ShapeDtypeStruct((micros, rows, width), jnp.bfloat16),
        in_specs=[whole, vmem, vmem, whole, whole, whole, vmem],
        out_specs=vmem,
        scratch_shapes=[
            half(micros, rows, width),
            half(own_rows, width),
            half(own_rows, width),
            full(own_rows, width),
            half(3, slots * hid, width),
            half(micros, rows, rows),
            half(micros, rows, rows),
            full(1, width),
            half(own_rows, width),
            half(own_rows, width),
            half(all_rows, width),
            half(own_rows, width),
            half(all_rows, width),
            half(all_rows, width),
            full(own_rows, width),
            full(own_rows, width),
            dma((slots, 6)), dma((slots, 6)),
            dma((2 * micros, PEERS)), dma((micros, PEERS)), dma((micros, PEERS)), dma((micros, PEERS)),
            dma((4,)), dma((4,)), dma((4,)),
            pltpu.SemaphoreType.REGULAR((3,)),
        ],
        compiler_params=pltpu.CompilerParams(
            collective_id=0, has_side_effects=True, vmem_limit_bytes=67_000_000
        ),
    )(
        tokens, norm_gains, router_cols.reshape(1, width),
        gate_weight[0, 0], up_weight[0, 0], down_weight[0, 0], jnp.swapaxes(expert_ids[0], 1, 2),
    )
    return result[None]


def gathered(tokens, norm_gains, router_cols, gate_weight, up_weight, down_weight, expert_ids):
    section = lax.axis_index("section")
    micros, rows, width = tokens.shape
    stacked = jnp.stack((gate_weight[0, 0], up_weight[0, 0], down_weight[0, 0]))
    panels = lax.all_gather(stacked, "fsdp", axis=1, tiled=True)
    gate, up, down = panels[0], panels[1], panels[2]

    def layer(hidden, routed):
        widened = hidden.astype(jnp.float32)
        mean_square = jnp.mean(widened * widened, axis=-1, keepdims=True)
        normed = (widened * lax.rsqrt(mean_square + EPS) * norm_gains[0]).astype(jnp.bfloat16)
        score = jax.nn.sigmoid(plain(normed, router_cols[0]))[:, 0]
        weight = jnp.where(jnp.any(routed == 0, axis=-1), score, jnp.zeros_like(score))
        activated = (jax.nn.silu(across(normed, gate)) * across(normed, up)).astype(jnp.bfloat16)
        return (widened + weight[:, None] * plain(activated, down)).astype(jnp.bfloat16)

    first = [layer(tokens[m], expert_ids[0, m]) for m in range(micros)]
    coming = [lax.ppermute(f, "section", [(0, 1)]) for f in first]
    second = [layer(coming[m], expert_ids[0, m]) for m in range(micros)]
    return jnp.where(section == 0, jnp.stack(first), jnp.stack(second))[None]


def solution(mesh):
    n = mesh.shape["fsdp"]

    def local(*args):
        hid = args[3].shape[2]
        if n == PEERS * PEERS and hid % (2 * BF16_ROWS) == 0:
            return grouped(n, *args)
        return gathered(*args)

    in_specs = (
        P(None, "fsdp", None),
        P("section", None),
        P("section", None, None),
        P("section", None, "fsdp", None),
        P("section", None, "fsdp", None),
        P("section", None, "fsdp", None),
        P("section", None, "fsdp", None),
    )
    out_specs = P("section", None, "fsdp", None)
    return jax.shard_map(local, mesh=mesh, in_specs=in_specs, out_specs=out_specs, check_vma=False)
```

```python
import functools

import jax
import jax.numpy as jnp
from jax import lax
from jax.experimental import pallas as pl
from jax.experimental.pallas import tpu as pltpu
from jax.sharding import PartitionSpec as P

MESH = pl.DeviceIdType.MESH
BF16_ROWS = 16
PEERS = 4
AHEAD = 10
CUTS = 2
FIRST = 0
EPS = 1e-05


def silu(v):
    return v / (1.0 + jnp.exp(-v))


def across(lhs, rhs):
    return lax.dot_general(lhs, rhs, (((1,), (1,)), ((), ())), preferred_element_type=jnp.float32)


def plain(lhs, rhs):
    return jnp.dot(lhs, rhs, preferred_element_type=jnp.float32)


def kernel(
    n, most,
    tokens, gain, router, gate, up, down, ids,
    out,
    base, held, hnext, early, weights, picked, picked_in, gain_in, outc, outc_in, xbuf, xnext, pbuf, psend, mine, across_part, rest,
    w_send, w_recv, x_send, x_recv, p_send, p_recv, o_send, o_recv, l_sem, go,
):
    sec = lax.axis_index("section")
    me = lax.axis_index("fsdp")
    micros, rows, width = tokens.shape
    hid = gate.shape[0]
    parts = hid // BF16_ROWS
    half = hid // parts
    pieces = most // BF16_ROWS
    group_rows = PEERS * most
    other = 1 - sec

    by_x = 1 - 2 * lax.rem(me, 2)
    by_y = 2 - 4 * lax.rem(lax.div(me, 2), 2)
    by_z = 4 - 8 * lax.rem(lax.div(me, 4), 2)
    by_far = 8 - 16 * lax.rem(lax.div(me, 8), 2)
    near = [me, me + by_z, me + by_far, me + by_z + by_far]
    cross = [me, me + by_y, me + by_z, me + by_y + by_z]
    peer = [a + sec * (b - a) for a, b in zip(near, cross)]
    at_x = me + by_x
    at_y = me + by_y
    far = me + by_far
    inner = lax.rem(lax.div(me, 4) + lax.div(me, 8), 2) == 1
    outer = jnp.logical_not(inner)

    barrier = pltpu.get_barrier_semaphore()
    met = [(sec, p) for p in [at_x, at_y, me + by_z, far, me + by_z + by_far, me + by_y + by_z]] + [(other, p) for p in cross]
    for device in met:
        pl.semaphore_signal(barrier, inc=1, device_id=device, device_id_type=MESH)

    own = (gate, up, down)
    chunks = [(a, h) for a in range(3) for h in range(parts)]

    fetch = [pltpu.make_async_copy(tokens, base, l_sem.at[3])]
    fetch += [pltpu.make_async_copy(own[a], weights.at[a, pl.ds(0, hid)], l_sem.at[a]) for a in range(3)]
    for copy in fetch:
        copy.start()

    def weight_copy(slot, chunk, target, send, recv, source_slot=None):
        a, h = chunks[chunk]
        span = pl.ds(h * half, half)
        if source_slot is None:
            src = own[a].at[span]
        else:
            src = weights.at[a, pl.ds(source_slot * hid + h * half, half)]
        return pltpu.make_async_remote_copy(
            src_ref=src,
            dst_ref=weights.at[a, pl.ds(slot * hid + h * half, half)],
            send_sem=w_send.at[send],
            recv_sem=w_recv.at[recv],
            device_id=(sec, target),
            device_id_type=MESH,
        )

    count = len(chunks)
    early_chunks = 2 * parts

    def group(k, chunk):
        return count + 2 * k + (1 if chunk >= early_chunks else 0)

    def x_copy(chunk, single=False):
        return weight_copy(1, chunk, at_x, 0, chunk if single else group(0, chunk))

    def y_copy(chunk, single=False):
        return weight_copy(2, chunk, at_y, 1, chunk if single else group(1, chunk))

    def own_copies(chunk):
        return [x_copy(chunk, chunk % 2 == 1), y_copy(chunk, chunk % 2 == 0)]

    def far_copy(chunk):
        return weight_copy(2, chunk, far, 1, chunk)

    def turn_copy(chunk):
        if chunk % 2 == 0:
            return weight_copy(3, chunk, at_x, 2, group(2, chunk), 2)
        return weight_copy(3, chunk, at_y, 3, group(2, chunk), 1)

    def far_turn_copy(chunk):
        return weight_copy(3, chunk, at_x, 2, group(2, chunk), 2)

    def sent(sems, k, ref, some):
        bulk = pltpu.make_async_remote_copy(
            src_ref=ref.at[pl.ds(0, some)], dst_ref=ref.at[pl.ds(0, some)],
            send_sem=sems.at[k], recv_sem=sems.at[k],
            device_id=(other, me), device_id_type=MESH,
        )
        bulk.wait_send()

    def got(sems, k, ref, some):
        bulk = pltpu.make_async_remote_copy(
            src_ref=ref.at[pl.ds(0, some)], dst_ref=ref.at[pl.ds(0, some)],
            send_sem=sems.at[k], recv_sem=sems.at[k],
            device_id=(other, me), device_id_type=MESH,
        )
        bulk.wait_recv()

    def block(m, j):
        return pl.ds((m * PEERS + j) * most, most)

    def share_of(m):
        return pl.ds(m * most, most)

    def token_copy(m, j):
        return pltpu.make_async_remote_copy(
            src_ref=xbuf.at[block(m, 0)], dst_ref=xbuf.at[block(m, j)],
            send_sem=x_send.at[j - 1], recv_sem=x_recv.at[m if j == 2 else micros],
            device_id=(sec, peer[j]), device_id_type=MESH,
        )

    def token_relay(m):
        return pltpu.make_async_remote_copy(
            src_ref=xbuf.at[block(m, PEERS - 2)], dst_ref=xbuf.at[block(m, PEERS - 1)],
            send_sem=x_send.at[0], recv_sem=x_recv.at[micros],
            device_id=(sec, peer[1]), device_id_type=MESH,
        )

    def onward_copy(m, j):
        return pltpu.make_async_remote_copy(
            src_ref=xnext.at[share_of(m)], dst_ref=xbuf.at[block(m, j)],
            send_sem=x_send.at[2], recv_sem=x_recv.at[m],
            device_id=(other, cross[j]), device_id_type=MESH,
        )

    def partial_copy(m, j):
        return pltpu.make_async_remote_copy(
            src_ref=psend.at[block(m, j)], dst_ref=pbuf.at[block(m, j)],
            send_sem=p_send.at[0], recv_sem=p_recv.at[m],
            device_id=(sec, peer[j]), device_id_type=MESH,
        )

    def piece(m, j, q):
        return pl.ds((m * PEERS + j) * most + q * BF16_ROWS, BF16_ROWS)

    def inward_copy(m, j, q):
        return pltpu.make_async_remote_copy(
            src_ref=psend.at[piece(m, j, q)], dst_ref=pbuf.at[piece(m, 5 - j, q)],
            send_sem=p_send.at[0], recv_sem=p_recv.at[micros + (m * 2 + 3 - j) * pieces + q],
            device_id=(sec, peer[1]), device_id_type=MESH,
        )

    def joined_copy(m, j, q):
        return pltpu.make_async_remote_copy(
            src_ref=psend.at[piece(m, j, q)], dst_ref=pbuf.at[piece(m, 0, q)],
            send_sem=p_send.at[0], recv_sem=p_recv.at[m],
            device_id=(sec, peer[j]), device_id_type=MESH,
        )

    def out_copy(m):
        return pltpu.make_async_copy(base.at[m], out.at[m], l_sem.at[m])

    def pass_copy(src, dst, k):
        return pltpu.make_async_remote_copy(
            src_ref=src, dst_ref=dst, send_sem=o_send.at[k], recv_sem=o_recv.at[k],
            device_id=(other, me), device_id_type=MESH,
        )

    pick_copy = pass_copy(picked, picked_in, 0)
    gain_copy = pass_copy(gain, gain_in, 1)
    held_copy = pass_copy(hnext, held, 2)
    outc_copy = pass_copy(outc, outc_in, 3)

    def norm(compact, scale):
        mean_square = jnp.mean(compact * compact, axis=-1, keepdims=True)
        return (compact * lax.rsqrt(mean_square + EPS) * scale).astype(jnp.bfloat16)

    def turned(picks):
        return jnp.transpose(picks.astype(jnp.float32))[0:most].astype(jnp.bfloat16)

    def merge(m, picks, compact, under):
        placed = plain(picks[m][:, 0:most], compact[m * most:(m + 1) * most, :])
        chosen = jnp.sum(picks[m].astype(jnp.float32), axis=1, keepdims=True) > 0.5
        return jnp.where(chosen, placed, under.astype(jnp.float32)).astype(jnp.bfloat16)

    with jax.named_scope("pick"):
        at_row = lax.broadcasted_iota(jnp.int32, (rows, rows), 0)
        at_col = lax.broadcasted_iota(jnp.int32, (rows, rows), 1)
        lower = jnp.where(at_row >= at_col, 1.0, 0.0).astype(jnp.bfloat16)
        for m in range(micros):
            named = jnp.sum(jnp.where(ids[m] == 0, 1.0, 0.0), axis=0, keepdims=True)
            spread = jnp.transpose(jnp.broadcast_to(named, (rows, rows)))
            rank = plain(lower, spread.astype(jnp.bfloat16))
            hit = (rank.astype(jnp.int32) - 1 == at_col) & (spread > 0.5)
            picked[m] = jnp.where(hit, 1.0, 0.0).astype(jnp.bfloat16)
        for copy in fetch:
            copy.wait()

    @pl.when(sec == 0)
    def _():
        for m in range(micros):
            compact = plain(turned(picked[m]), base[m])
            held[share_of(m), :] = compact.astype(jnp.bfloat16)
            xbuf[block(m, 0), :] = norm(compact, gain[...])

    with jax.named_scope("bar"):
        pl.semaphore_wait(barrier, len(met))

    @pl.when(sec == 0)
    def _():
        for m in range(micros):
            for j in range(PEERS - 2, 0, -1):
                token_copy(m, j).start()
        for c in range(len(chunks)):
            for copy in own_copies(c):
                copy.start()
        pick_copy.start()
        pick_copy.wait_recv()
        gain_copy.wait_recv()
        sent(x_send, 1, xbuf, micros * most)
        pl.semaphore_signal(go.at[0], inc=1, device_id=(other, me), device_id_type=MESH)
        for m in range(micros):
            early[share_of(m), :] = plain(turned(picked_in[m]), base[m])

        with jax.named_scope("xrelay"):
            for m in range(micros):
                token_copy(m, PEERS - 2).wait_recv()
                token_relay(m).start()
        for c in range(len(chunks)):
            with jax.named_scope("wrelay"):
                (y_copy if c % 2 == 0 else x_copy)(c, True).wait_recv()
            turn_copy(c).start()
        with jax.named_scope("xsent"):
            sent(w_send, 2, weights.at[0], 3 * hid // 2)
        pl.semaphore_signal(go.at[1], inc=1, device_id=(other, me), device_id_type=MESH)

    @pl.when(sec == 1)
    def _():
        for c in range(FIRST):
            far_copy(c).start()
        gain_copy.start()
        pick_copy.start()
        pick_copy.wait_recv()
        with jax.named_scope("go0"):
            pl.semaphore_wait(go.at[0], 1)
        for c in range(FIRST, AHEAD):
            far_copy(c).start()
        with jax.named_scope("go1"):
            pl.semaphore_wait(go.at[1], 1)
        for c in range(AHEAD):
            x_copy(c).start()
            with jax.named_scope("frelay"):
                far_copy(c).wait_recv()
            far_turn_copy(c).start()
        for c in range(AHEAD, len(chunks)):
            x_copy(c).start()
        with jax.named_scope("go2"):
            pl.semaphore_wait(go.at[2], 1)
        for c in range(AHEAD, len(chunks)):
            far_copy(c).start()
        for c in range(AHEAD, len(chunks)):
            with jax.named_scope("frelay"):
                far_copy(c).wait_recv()
            far_turn_copy(c).start()

    def wait_weights(late, kinds):
        @pl.when(sec == 0)
        def _():
            got(w_recv, count + late, weights.at[0], kinds * hid // 2)
            got(w_recv, count + 2 + late, weights.at[0], kinds * hid // 2)
            got(w_recv, count + 4 + late, weights.at[0], kinds * hid)

        @pl.when(sec == 1)
        def _():
            got(w_recv, count + late, weights.at[0], kinds * hid)
            got(w_recv, count + 4 + late, weights.at[0], kinds * hid)

    with jax.named_scope("ww"):
        wait_weights(0, 2)

    @pl.when(sec == 0)
    def _():
        with jax.named_scope("wtok"):
            got(x_recv, micros, xbuf, 2 * micros * most)

    for m in range(micros):
        @pl.when(sec == 1)
        def _():
            with jax.named_scope("won"):
                got(x_recv, m, xbuf, PEERS * most)

        with jax.named_scope("gu"):
            x = xbuf[pl.ds(m * group_rows, group_rows), :]
            activated = (silu(across(x, weights[0])) * across(x, weights[1])).astype(jnp.bfloat16)
        if m == 0:
            with jax.named_scope("ww2"):
                wait_weights(1, 1)
        with jax.named_scope("down"):
            partial = plain(activated, weights[2])
            mine[share_of(m), :] = partial[0:most]
            psend[pl.ds(m * group_rows, group_rows), :] = partial.astype(jnp.bfloat16)
        @pl.when(sec == 0)
        def _():
            across_part[pl.ds(m * 2 * most, 2 * most), :] = partial[2 * most:4 * most]

            @pl.when(outer)
            def _():
                for q in range(pieces):
                    for j in (3, 2):
                        inward_copy(m, j, q).start()

            if m == micros - 1:
                for k in range(micros):
                    partial_copy(k, 1).start()

        @pl.when(sec == 1)
        def _():
            for j in range(PEERS - 1, 0, -1):
                partial_copy(m, j).start()

    @pl.when((sec == 0) & inner)
    def _():
        for m in range(micros):
            for q in range(pieces):
                for j in (2, 3):
                    with jax.named_scope("wearly"):
                        inward_copy(m, 5 - j, q).wait_recv()
                    mine_too = across_part[pl.ds((m * 2 + j - 2) * most + q * BF16_ROWS, BF16_ROWS), :]
                    joined = mine_too + pbuf[piece(m, j, q), :].astype(jnp.float32)
                    psend[piece(m, j, q), :] = joined.astype(jnp.bfloat16)
                    joined_copy(m, j, q).start()
    @pl.when(sec == 1)
    def _():
        held_copy.wait_recv()
        outc_copy.wait_recv()
        for m in range(micros):
            base[m] = merge(m, picked_in, outc_in, base[m])

    for m in range(micros):
        span = share_of(m)
        with jax.named_scope("wpart"):
            score = jnp.sum(xbuf[block(m, 0), :].astype(jnp.float32) * router[...].astype(jnp.float32), axis=1, keepdims=True)
            share = 1.0 / (1.0 + jnp.exp(-score))
            @pl.when(sec == 0)
            def _():
                got(p_recv, m, pbuf, 2 * most)
                if m == 0:
                    pl.semaphore_signal(go.at[2], inc=1, device_id=(other, me), device_id_type=MESH)

            @pl.when(sec == 1)
            def _():
                got(p_recv, m, pbuf, 3 * most)

            update = mine[span, :] + pbuf[block(m, 1), :].astype(jnp.float32)

            @pl.when(sec == 0)
            def _():
                rest[...] = pbuf[block(m, 0), :].astype(jnp.float32)

            @pl.when(sec == 1)
            def _():
                rest[...] = pbuf[block(m, 2), :].astype(jnp.float32) + pbuf[block(m, 3), :].astype(jnp.float32)

            update = update + rest[...]
        outc[span, :] = (held[span, :].astype(jnp.float32) + share * update).astype(jnp.bfloat16)

        @pl.when(sec == 0)
        def _():
            with jax.named_scope("next"):
                again = plain(turned(picked_in[m]), picked[m][:, 0:most])
                changed = jnp.sum(again, axis=1, keepdims=True) > 0.5
                following = jnp.where(changed, plain(again.astype(jnp.bfloat16), outc[span, :]), early[span, :])
                xnext[span, :] = norm(following, gain_in[...])
                hnext[span, :] = following.astype(jnp.bfloat16)
            for j in range(PEERS - 1, -1, -1):
                onward_copy(m, j).start()

        @pl.when(sec == 1)
        def _():
            base[m] = merge(m, picked, outc, base[m])
            out_copy(m).start()

    @pl.when(sec == 0)
    def _():
        held_copy.start()
        outc_copy.start()
        for m in range(micros):
            base[m] = merge(m, picked, outc, base[m])
            out_copy(m).start()

    sent(w_send, 0, weights.at[0], 3 * hid)
    sent(w_send, 1, weights.at[0], 3 * hid)
    pick_copy.wait_send()
    for m in range(micros):
        out_copy(m).wait()
    sent(p_send, 0, psend, 3 * micros * most)

    @pl.when(sec == 0)
    def _():
        sent(w_send, 3, weights.at[0], 3 * hid // 2)
        held_copy.wait_send()
        outc_copy.wait_send()
        sent(x_send, 0, xbuf, 2 * micros * most)
        sent(x_send, 2, xbuf, PEERS * micros * most)

    @pl.when(sec == 1)
    def _():
        sent(w_send, 2, weights.at[0], 3 * hid)
        gain_copy.wait_send()


def grouped(n, tokens, norm_gains, router_cols, gate_weight, up_weight, down_weight, expert_ids):
    micros, rows, width = tokens.shape
    hid = gate_weight.shape[2]
    most = rows // 4
    slots = n // PEERS
    own_rows = micros * most
    chunks = 3 * (hid // BF16_ROWS)
    pieces = most // BF16_ROWS
    all_rows = PEERS * own_rows
    dma = pltpu.SemaphoreType.DMA
    vmem = pl.BlockSpec(memory_space=pltpu.VMEM)
    whole = pl.BlockSpec(memory_space=pltpu.HBM)
    half = lambda *shape: pltpu.VMEM(shape, jnp.bfloat16)
    full = lambda *shape: pltpu.VMEM(shape, jnp.float32)
    result = pl.pallas_call(
        functools.partial(kernel, n, most),
        out_shape=jax.ShapeDtypeStruct((micros, rows, width), jnp.bfloat16),
        in_specs=[whole, vmem, vmem, whole, whole, whole, vmem],
        out_specs=whole,
        scratch_shapes=[
            half(micros, rows, width),
            half(own_rows, width),
            half(own_rows, width),
            full(own_rows, width),
            half(3, slots * hid, width),
            half(micros, rows, rows),
            half(micros, rows, rows),
            full(1, width),
            half(own_rows, width),
            half(own_rows, width),
            half(all_rows, width),
            half(own_rows, width),
            half(all_rows, width),
            half(all_rows, width),
            full(own_rows, width),
            full(2 * own_rows, width),
            full(most, width),
            dma((4,)), dma((chunks + 6,)),
            dma((3,)), dma((micros + 1,)), dma((1,)), dma((micros + 2 * micros * pieces,)),
            dma((4,)), dma((4,)), dma((4,)),
            pltpu.SemaphoreType.REGULAR((3,)),
        ],
        compiler_params=pltpu.CompilerParams(
            collective_id=0, has_side_effects=True, vmem_limit_bytes=67_000_000
        ),
    )(
        tokens, norm_gains, router_cols.reshape(1, width),
        gate_weight[0, 0], up_weight[0, 0], down_weight[0, 0], jnp.swapaxes(expert_ids[0], 1, 2),
    )
    return finish(result)[None]


def finish_kernel(src, dst, hold, i_sem, o_sem):
    micros, rows, width = src.shape
    step = rows // CUTS
    parts = [(m, pl.ds(c * step, step), m * CUTS + c) for m in range(micros) for c in range(CUTS)]
    come = [pltpu.make_async_copy(src.at[m, r], hold.at[m, r], i_sem.at[k]) for m, r, k in parts]
    leave = [pltpu.make_async_copy(hold.at[m, r], dst.at[m, r], o_sem.at[k]) for m, r, k in parts]
    for copy in come:
        copy.start()
    for a, b in zip(come, leave):
        a.wait()
        b.start()
    for copy in leave:
        copy.wait()


def finish(result):
    whole = pl.BlockSpec(memory_space=pltpu.HBM)
    return pl.pallas_call(
        finish_kernel,
        out_shape=jax.ShapeDtypeStruct(result.shape, result.dtype),
        in_specs=[whole],
        out_specs=whole,
        scratch_shapes=[pltpu.VMEM(result.shape, result.dtype), pltpu.SemaphoreType.DMA((2 * CUTS,)), pltpu.SemaphoreType.DMA((2 * CUTS,))],
    )(result)


def gathered(tokens, norm_gains, router_cols, gate_weight, up_weight, down_weight, expert_ids):
    section = lax.axis_index("section")
    micros, rows, width = tokens.shape
    stacked = jnp.stack((gate_weight[0, 0], up_weight[0, 0], down_weight[0, 0]))
    panels = lax.all_gather(stacked, "fsdp", axis=1, tiled=True)
    gate, up, down = panels[0], panels[1], panels[2]

    def layer(hidden, routed):
        widened = hidden.astype(jnp.float32)
        mean_square = jnp.mean(widened * widened, axis=-1, keepdims=True)
        normed = (widened * lax.rsqrt(mean_square + EPS) * norm_gains[0]).astype(jnp.bfloat16)
        score = jax.nn.sigmoid(plain(normed, router_cols[0]))[:, 0]
        weight = jnp.where(jnp.any(routed == 0, axis=-1), score, jnp.zeros_like(score))
        activated = (jax.nn.silu(across(normed, gate)) * across(normed, up)).astype(jnp.bfloat16)
        return (widened + weight[:, None] * plain(activated, down)).astype(jnp.bfloat16)

    first = [layer(tokens[m], expert_ids[0, m]) for m in range(micros)]
    coming = [lax.ppermute(f, "section", [(0, 1)]) for f in first]
    second = [layer(coming[m], expert_ids[0, m]) for m in range(micros)]
    return jnp.where(section == 0, jnp.stack(first), jnp.stack(second))[None]


def solution(mesh):
    n = mesh.shape["fsdp"]

    def local(*args):
        hid = args[3].shape[2]
        if n == PEERS * PEERS and hid % (2 * BF16_ROWS) == 0:
            return grouped(n, *args)
        return gathered(*args)

    in_specs = (
        P(None, "fsdp", None),
        P("section", None),
        P("section", None, None),
        P("section", None, "fsdp", None),
        P("section", None, "fsdp", None),
        P("section", None, "fsdp", None),
        P("section", None, "fsdp", None),
    )
    out_specs = P("section", None, "fsdp", None)
    return jax.shard_map(local, mesh=mesh, in_specs=in_specs, out_specs=out_specs, check_vma=False)
```

```python
import functools

import jax
import jax.numpy as jnp
from jax import lax
from jax.experimental import pallas as pl
from jax.experimental.pallas import tpu as pltpu
from jax.sharding import PartitionSpec as P

MESH = pl.DeviceIdType.MESH
BF16_ROWS = 16
PEERS = 4
AHEAD = 10
LEFT = 4
CUTS = 2
FIRST = 0
EPS = 1e-05


def silu(v):
    return v / (1.0 + jnp.exp(-v))


def across(lhs, rhs):
    return lax.dot_general(lhs, rhs, (((1,), (1,)), ((), ())), preferred_element_type=jnp.float32)


def plain(lhs, rhs):
    return jnp.dot(lhs, rhs, preferred_element_type=jnp.float32)


def kernel(
    n, most,
    tokens, gain_at, router_at, gate, up, down, ids_at,
    out,
    gain, router, ids, base, held, hnext, early, weights, picked, picked_in, gain_in, outc, outc_in, xbuf, xnext, pbuf, psend, mine, across_part, rest,
    w_send, w_recv, x_send, x_recv, p_send, p_recv, o_send, o_recv, l_sem, go,
):
    sec = lax.axis_index("section")
    me = lax.axis_index("fsdp")
    micros, rows, width = tokens.shape
    hid = gate.shape[0]
    parts = hid // BF16_ROWS
    half = hid // parts
    pieces = most // BF16_ROWS
    group_rows = PEERS * most
    other = 1 - sec

    by_x = 1 - 2 * lax.rem(me, 2)
    by_y = 2 - 4 * lax.rem(lax.div(me, 2), 2)
    by_z = 4 - 8 * lax.rem(lax.div(me, 4), 2)
    by_far = 8 - 16 * lax.rem(lax.div(me, 8), 2)
    near = [me, me + by_z, me + by_far, me + by_z + by_far]
    cross = [me, me + by_y, me + by_z, me + by_y + by_z]
    peer = [a + sec * (b - a) for a, b in zip(near, cross)]
    at_x = me + by_x
    at_y = me + by_y
    far = me + by_far
    inner = lax.rem(lax.div(me, 4) + lax.div(me, 8), 2) == 1
    outer = jnp.logical_not(inner)

    barrier = pltpu.get_barrier_semaphore()
    met = [(sec, p) for p in [at_x, at_y, me + by_z, far, me + by_z + by_far, me + by_y + by_z]] + [(other, p) for p in cross]
    for device in met:
        pl.semaphore_signal(barrier, inc=1, device_id=device, device_id_type=MESH)

    own = (gate, up, down)
    chunks = [(a, h) for a in range(3) for h in range(parts)]

    small = [pltpu.make_async_copy(src, dst, l_sem.at[4 + k]) for k, (src, dst) in enumerate([(ids_at, ids), (gain_at, gain), (router_at, router)])]
    fetch = [pltpu.make_async_copy(tokens, base, l_sem.at[3])]
    fetch += [pltpu.make_async_copy(own[a], weights.at[a, pl.ds(0, hid)], l_sem.at[a]) for a in range(3)]
    for copy in small + fetch[:1]:
        copy.start()

    def weight_copy(slot, chunk, target, send, recv, source_slot=None):
        a, h = chunks[chunk]
        span = pl.ds(h * half, half)
        if source_slot is None:
            src = own[a].at[span]
        else:
            src = weights.at[a, pl.ds(source_slot * hid + h * half, half)]
        return pltpu.make_async_remote_copy(
            src_ref=src,
            dst_ref=weights.at[a, pl.ds(slot * hid + h * half, half)],
            send_sem=w_send.at[send],
            recv_sem=w_recv.at[recv],
            device_id=(sec, target),
            device_id_type=MESH,
        )

    count = len(chunks)
    early_chunks = 2 * parts

    def group(k, chunk):
        return count + 2 * k + (1 if chunk >= early_chunks else 0)

    def x_copy(chunk, single=False):
        return weight_copy(1, chunk, at_x, 0, chunk if single else group(0, chunk))

    def y_copy(chunk, single=False):
        return weight_copy(2, chunk, at_y, 1, chunk if single else group(1, chunk))

    def own_copies(chunk):
        return [x_copy(chunk, chunk % 2 == 1), y_copy(chunk, chunk % 2 == 0)]

    def far_copy(chunk):
        return weight_copy(2, chunk, far, 1, chunk)

    def turn_copy(chunk):
        if chunk % 2 == 0:
            return weight_copy(3, chunk, at_x, 2 if chunk < 2 * LEFT else 4, group(2, chunk), 2)
        return weight_copy(3, chunk, at_y, 3, group(2, chunk), 1)

    def far_turn_copy(chunk):
        return weight_copy(3, chunk, at_x, 2, group(2, chunk), 2)

    def sent(sems, k, ref, some):
        bulk = pltpu.make_async_remote_copy(
            src_ref=ref.at[pl.ds(0, some)], dst_ref=ref.at[pl.ds(0, some)],
            send_sem=sems.at[k], recv_sem=sems.at[k],
            device_id=(other, me), device_id_type=MESH,
        )
        bulk.wait_send()

    def got(sems, k, ref, some):
        bulk = pltpu.make_async_remote_copy(
            src_ref=ref.at[pl.ds(0, some)], dst_ref=ref.at[pl.ds(0, some)],
            send_sem=sems.at[k], recv_sem=sems.at[k],
            device_id=(other, me), device_id_type=MESH,
        )
        bulk.wait_recv()

    def block(m, j):
        return pl.ds((m * PEERS + j) * most, most)

    def share_of(m):
        return pl.ds(m * most, most)

    def token_copy(m, j):
        return pltpu.make_async_remote_copy(
            src_ref=xbuf.at[block(m, 0)], dst_ref=xbuf.at[block(m, j)],
            send_sem=x_send.at[j - 1], recv_sem=x_recv.at[m if j == 2 else micros],
            device_id=(sec, peer[j]), device_id_type=MESH,
        )

    def token_relay(m):
        return pltpu.make_async_remote_copy(
            src_ref=xbuf.at[block(m, PEERS - 2)], dst_ref=xbuf.at[block(m, PEERS - 1)],
            send_sem=x_send.at[0], recv_sem=x_recv.at[micros],
            device_id=(sec, peer[1]), device_id_type=MESH,
        )

    def onward_copy(m, j, q):
        return pltpu.make_async_remote_copy(
            src_ref=xnext.at[pl.ds(m * most + q * BF16_ROWS, BF16_ROWS)], dst_ref=xbuf.at[piece(m, j, q)],
            send_sem=x_send.at[2], recv_sem=x_recv.at[m],
            device_id=(other, cross[j]), device_id_type=MESH,
        )

    def partial_copy(m, j):
        return pltpu.make_async_remote_copy(
            src_ref=psend.at[block(m, j)], dst_ref=pbuf.at[block(m, j)],
            send_sem=p_send.at[0], recv_sem=p_recv.at[m],
            device_id=(sec, peer[j]), device_id_type=MESH,
        )

    def piece(m, j, q):
        return pl.ds((m * PEERS + j) * most + q * BF16_ROWS, BF16_ROWS)

    def inward_copy(m, j, q):
        return pltpu.make_async_remote_copy(
            src_ref=psend.at[piece(m, j, q)], dst_ref=pbuf.at[piece(m, 5 - j, q)],
            send_sem=p_send.at[0], recv_sem=p_recv.at[micros + (m * 2 + 3 - j) * pieces + q],
            device_id=(sec, peer[1]), device_id_type=MESH,
        )

    def share_copy(m, j, q):
        return pltpu.make_async_remote_copy(
            src_ref=psend.at[piece(m, j, q)], dst_ref=pbuf.at[piece(m, j, q)],
            send_sem=p_send.at[0], recv_sem=p_recv.at[m],
            device_id=(sec, peer[j]), device_id_type=MESH,
        )

    def joined_copy(m, j, q):
        return pltpu.make_async_remote_copy(
            src_ref=psend.at[piece(m, j, q)], dst_ref=pbuf.at[piece(m, 0, q)],
            send_sem=p_send.at[0], recv_sem=p_recv.at[m],
            device_id=(sec, peer[j]), device_id_type=MESH,
        )

    def out_copy(m):
        return pltpu.make_async_copy(base.at[m], out.at[m], l_sem.at[m])

    def pass_copy(src, dst, k):
        return pltpu.make_async_remote_copy(
            src_ref=src, dst_ref=dst, send_sem=o_send.at[k], recv_sem=o_recv.at[k],
            device_id=(other, me), device_id_type=MESH,
        )

    pick_copy = pass_copy(picked, picked_in, 0)
    gain_copy = pass_copy(gain, gain_in, 1)
    held_copy = pass_copy(hnext, held, 2)
    outc_copy = pass_copy(outc, outc_in, 3)

    def norm(compact, scale):
        mean_square = jnp.mean(compact * compact, axis=-1, keepdims=True)
        return (compact * lax.rsqrt(mean_square + EPS) * scale).astype(jnp.bfloat16)

    def turned(picks):
        return jnp.transpose(picks.astype(jnp.float32))[0:most].astype(jnp.bfloat16)

    def merge(m, picks, compact, under):
        placed = plain(picks[m][:, 0:most], compact[m * most:(m + 1) * most, :])
        chosen = jnp.sum(picks[m].astype(jnp.float32), axis=1, keepdims=True) > 0.5
        return jnp.where(chosen, placed, under.astype(jnp.float32)).astype(jnp.bfloat16)

    with jax.named_scope("pick"):
        for copy in small:
            copy.wait()
        at_row = lax.broadcasted_iota(jnp.int32, (rows, rows), 0)
        at_col = lax.broadcasted_iota(jnp.int32, (rows, rows), 1)
        lower = jnp.where(at_row >= at_col, 1.0, 0.0).astype(jnp.bfloat16)
        for m in range(micros):
            named = jnp.sum(jnp.where(ids[m] == 0, 1.0, 0.0), axis=0, keepdims=True)
            spread = jnp.transpose(jnp.broadcast_to(named, (rows, rows)))
            rank = plain(lower, spread.astype(jnp.bfloat16))
            hit = (rank.astype(jnp.int32) - 1 == at_col) & (spread > 0.5)
            picked[m] = jnp.where(hit, 1.0, 0.0).astype(jnp.bfloat16)
        fetch[0].wait()
    for copy in fetch[1:]:
        copy.start()

    @pl.when(sec == 0)
    def _():
        for m in range(micros):
            compact = plain(turned(picked[m]), base[m])
            held[share_of(m), :] = compact.astype(jnp.bfloat16)
            xbuf[block(m, 0), :] = norm(compact, gain[...])

    with jax.named_scope("bar"):
        pl.semaphore_wait(barrier, len(met))

    @pl.when(sec == 0)
    def _():
        for m in range(micros):
            for j in range(PEERS - 2, 0, -1):
                token_copy(m, j).start()
        for c in range(len(chunks)):
            for copy in own_copies(c):
                copy.start()
        pick_copy.start()
        pick_copy.wait_recv()
        gain_copy.wait_recv()
        sent(x_send, 1, xbuf, micros * most)
        pl.semaphore_signal(go.at[0], inc=1, device_id=(other, me), device_id_type=MESH)
        for m in range(micros):
            early[share_of(m), :] = plain(turned(picked_in[m]), base[m])

        with jax.named_scope("xrelay"):
            for m in range(micros):
                token_copy(m, PEERS - 2).wait_recv()
                token_relay(m).start()
        for c in range(len(chunks)):
            with jax.named_scope("wrelay"):
                (y_copy if c % 2 == 0 else x_copy)(c, True).wait_recv()
            turn_copy(c).start()
        with jax.named_scope("xsent"):
            sent(w_send, 2, weights.at[0], LEFT * half)
        pl.semaphore_signal(go.at[1], inc=1, device_id=(other, me), device_id_type=MESH)

    @pl.when(sec == 1)
    def _():
        for c in range(FIRST):
            far_copy(c).start()
        gain_copy.start()
        pick_copy.start()
        pick_copy.wait_recv()
        with jax.named_scope("go0"):
            pl.semaphore_wait(go.at[0], 1)
        for c in range(FIRST, AHEAD):
            far_copy(c).start()
        with jax.named_scope("go1"):
            pl.semaphore_wait(go.at[1], 1)
        for c in range(AHEAD):
            x_copy(c).start()
            with jax.named_scope("frelay"):
                far_copy(c).wait_recv()
            far_turn_copy(c).start()
        for c in range(AHEAD, len(chunks)):
            x_copy(c).start()
        with jax.named_scope("go2"):
            pl.semaphore_wait(go.at[2], 1)
        for c in range(AHEAD, len(chunks)):
            far_copy(c).start()
        for c in range(AHEAD, len(chunks)):
            with jax.named_scope("frelay"):
                far_copy(c).wait_recv()
            far_turn_copy(c).start()

    def wait_weights(late, kinds):
        @pl.when(sec == 0)
        def _():
            got(w_recv, count + late, weights.at[0], kinds * hid // 2)
            got(w_recv, count + 2 + late, weights.at[0], kinds * hid // 2)
            got(w_recv, count + 4 + late, weights.at[0], kinds * hid)

        @pl.when(sec == 1)
        def _():
            got(w_recv, count + late, weights.at[0], kinds * hid)
            got(w_recv, count + 4 + late, weights.at[0], kinds * hid)

    for copy in fetch[1:]:
        copy.wait()
    with jax.named_scope("ww"):
        wait_weights(0, 2)

    @pl.when(sec == 0)
    def _():
        with jax.named_scope("wtok"):
            got(x_recv, micros, xbuf, 2 * micros * most)

    for m in range(micros):
        @pl.when(sec == 1)
        def _():
            with jax.named_scope("won"):
                got(x_recv, m, xbuf, PEERS * most)

        with jax.named_scope("gu"):
            x = xbuf[pl.ds(m * group_rows, group_rows), :]
            activated = (silu(across(x, weights[0])) * across(x, weights[1])).astype(jnp.bfloat16)
        if m == 0:
            with jax.named_scope("ww2"):
                wait_weights(1, 1)
        with jax.named_scope("down"):
            partial = plain(activated, weights[2])
            mine[share_of(m), :] = partial[0:most]
            psend[pl.ds(m * group_rows, group_rows), :] = partial.astype(jnp.bfloat16)
        @pl.when(sec == 0)
        def _():
            across_part[pl.ds(m * 2 * most, 2 * most), :] = partial[2 * most:4 * most]

            @pl.when(outer)
            def _():
                for q in range(pieces):
                    for j in (3, 2):
                        inward_copy(m, j, q).start()

            if m == micros - 1:
                for k in range(micros):
                    partial_copy(k, 1).start()

        @pl.when(sec == 1)
        def _():
            for j in range(PEERS - 1, 0, -1):
                for q in range(pieces):
                    share_copy(m, j, q).start()

    @pl.when((sec == 0) & inner)
    def _():
        for m in range(micros):
            for q in range(pieces):
                for j in (2, 3):
                    with jax.named_scope("wearly"):
                        inward_copy(m, 5 - j, q).wait_recv()
                    mine_too = across_part[pl.ds((m * 2 + j - 2) * most + q * BF16_ROWS, BF16_ROWS), :]
                    joined = mine_too + pbuf[piece(m, j, q), :].astype(jnp.float32)
                    psend[piece(m, j, q), :] = joined.astype(jnp.bfloat16)
                    joined_copy(m, j, q).start()
    @pl.when(sec == 1)
    def _():
        held_copy.wait_recv()
        outc_copy.wait_recv()
        for m in range(micros):
            base[m] = merge(m, picked_in, outc_in, base[m])

    for m in range(micros):
        span = share_of(m)
        with jax.named_scope("wpart"):
            score = jnp.sum(xbuf[block(m, 0), :].astype(jnp.float32) * router[...].astype(jnp.float32), axis=1, keepdims=True)
            share = 1.0 / (1.0 + jnp.exp(-score))
            @pl.when(sec == 0)
            def _():
                got(p_recv, m, pbuf, 2 * most)
                if m == 0:
                    pl.semaphore_signal(go.at[2], inc=1, device_id=(other, me), device_id_type=MESH)

            @pl.when(sec == 1)
            def _():
                got(p_recv, m, pbuf, 3 * most)

            update = mine[span, :] + pbuf[block(m, 1), :].astype(jnp.float32)

            @pl.when(sec == 0)
            def _():
                rest[...] = pbuf[block(m, 0), :].astype(jnp.float32)

            @pl.when(sec == 1)
            def _():
                rest[...] = pbuf[block(m, 2), :].astype(jnp.float32) + pbuf[block(m, 3), :].astype(jnp.float32)

            update = update + rest[...]
        outc[span, :] = (held[span, :].astype(jnp.float32) + share * update).astype(jnp.bfloat16)

        @pl.when(sec == 0)
        def _():
            with jax.named_scope("next"):
                again = plain(turned(picked_in[m]), picked[m][:, 0:most])
                changed = jnp.sum(again, axis=1, keepdims=True) > 0.5
                following = jnp.where(changed, plain(again.astype(jnp.bfloat16), outc[span, :]), early[span, :])
                xnext[span, :] = norm(following, gain_in[...])
                hnext[span, :] = following.astype(jnp.bfloat16)
            for j in range(PEERS - 1, -1, -1):
                for q in range(pieces):
                    onward_copy(m, j, q).start()

        @pl.when(sec == 1)
        def _():
            base[m] = merge(m, picked, outc, base[m])
            out_copy(m).start()

    @pl.when(sec == 0)
    def _():
        held_copy.start()
        outc_copy.start()
        for m in range(micros):
            base[m] = merge(m, picked, outc, base[m])
            out_copy(m).start()

    sent(w_send, 0, weights.at[0], 3 * hid)
    sent(w_send, 1, weights.at[0], 3 * hid)
    pick_copy.wait_send()
    for m in range(micros):
        out_copy(m).wait()
    sent(p_send, 0, psend, 3 * micros * most)

    @pl.when(sec == 0)
    def _():
        sent(w_send, 3, weights.at[0], 3 * hid // 2)
        sent(w_send, 4, weights.at[0], (count // 2 - LEFT) * half)
        held_copy.wait_send()
        outc_copy.wait_send()
        sent(x_send, 0, xbuf, 2 * micros * most)
        sent(x_send, 2, xbuf, PEERS * micros * most)

    @pl.when(sec == 1)
    def _():
        sent(w_send, 2, weights.at[0], 3 * hid)
        gain_copy.wait_send()


def grouped(n, tokens, norm_gains, router_cols, gate_weight, up_weight, down_weight, expert_ids):
    micros, rows, width = tokens.shape
    hid = gate_weight.shape[2]
    most = rows // 4
    slots = n // PEERS
    own_rows = micros * most
    chunks = 3 * (hid // BF16_ROWS)
    pieces = most // BF16_ROWS
    all_rows = PEERS * own_rows
    dma = pltpu.SemaphoreType.DMA
    whole = pl.BlockSpec(memory_space=pltpu.HBM)
    half = lambda *shape: pltpu.VMEM(shape, jnp.bfloat16)
    full = lambda *shape: pltpu.VMEM(shape, jnp.float32)
    result = pl.pallas_call(
        functools.partial(kernel, n, most),
        out_shape=jax.ShapeDtypeStruct((micros, rows, width), jnp.bfloat16),
        in_specs=[whole] * 7,
        out_specs=whole,
        scratch_shapes=[
            full(1, width),
            half(1, width),
            pltpu.VMEM(expert_ids.shape[1:2] + expert_ids.shape[3:1:-1], jnp.int32),
            half(micros, rows, width),
            half(own_rows, width),
            half(own_rows, width),
            full(own_rows, width),
            half(3, slots * hid, width),
            half(micros, rows, rows),
            half(micros, rows, rows),
            full(1, width),
            half(own_rows, width),
            half(own_rows, width),
            half(all_rows, width),
            half(own_rows, width),
            half(all_rows, width),
            half(all_rows, width),
            full(own_rows, width),
            full(2 * own_rows, width),
            full(most, width),
            dma((5,)), dma((chunks + 6,)),
            dma((3,)), dma((micros + 1,)), dma((1,)), dma((micros + 2 * micros * pieces,)),
            dma((4,)), dma((4,)), dma((7,)),
            pltpu.SemaphoreType.REGULAR((3,)),
        ],
        compiler_params=pltpu.CompilerParams(
            collective_id=0, has_side_effects=True, vmem_limit_bytes=67_000_000
        ),
    )(
        tokens, norm_gains, router_cols.reshape(1, width),
        gate_weight[0, 0], up_weight[0, 0], down_weight[0, 0], jnp.swapaxes(expert_ids[0], 1, 2),
    )
    return finish(result)[None]


def finish_kernel(src, dst, hold, i_sem, o_sem):
    micros, rows, width = src.shape
    step = rows // CUTS
    parts = [(m, pl.ds(c * step, step), m * CUTS + c) for m in range(micros) for c in range(CUTS)]
    come = [pltpu.make_async_copy(src.at[m, r], hold.at[m, r], i_sem.at[k]) for m, r, k in parts]
    leave = [pltpu.make_async_copy(hold.at[m, r], dst.at[m, r], o_sem.at[k]) for m, r, k in parts]
    for copy in come:
        copy.start()
    for a, b in zip(come, leave):
        a.wait()
        b.start()
    for copy in leave:
        copy.wait()


def finish(result):
    whole = pl.BlockSpec(memory_space=pltpu.HBM)
    return pl.pallas_call(
        finish_kernel,
        out_shape=jax.ShapeDtypeStruct(result.shape, result.dtype),
        in_specs=[whole],
        out_specs=whole,
        scratch_shapes=[pltpu.VMEM(result.shape, result.dtype), pltpu.SemaphoreType.DMA((2 * CUTS,)), pltpu.SemaphoreType.DMA((2 * CUTS,))],
    )(result)


def gathered(tokens, norm_gains, router_cols, gate_weight, up_weight, down_weight, expert_ids):
    section = lax.axis_index("section")
    micros, rows, width = tokens.shape
    stacked = jnp.stack((gate_weight[0, 0], up_weight[0, 0], down_weight[0, 0]))
    panels = lax.all_gather(stacked, "fsdp", axis=1, tiled=True)
    gate, up, down = panels[0], panels[1], panels[2]

    def layer(hidden, routed):
        widened = hidden.astype(jnp.float32)
        mean_square = jnp.mean(widened * widened, axis=-1, keepdims=True)
        normed = (widened * lax.rsqrt(mean_square + EPS) * norm_gains[0]).astype(jnp.bfloat16)
        score = jax.nn.sigmoid(plain(normed, router_cols[0]))[:, 0]
        weight = jnp.where(jnp.any(routed == 0, axis=-1), score, jnp.zeros_like(score))
        activated = (jax.nn.silu(across(normed, gate)) * across(normed, up)).astype(jnp.bfloat16)
        return (widened + weight[:, None] * plain(activated, down)).astype(jnp.bfloat16)

    first = [layer(tokens[m], expert_ids[0, m]) for m in range(micros)]
    coming = [lax.ppermute(f, "section", [(0, 1)]) for f in first]
    second = [layer(coming[m], expert_ids[0, m]) for m in range(micros)]
    return jnp.where(section == 0, jnp.stack(first), jnp.stack(second))[None]


def solution(mesh):
    n = mesh.shape["fsdp"]

    def local(*args):
        hid = args[3].shape[2]
        if n == PEERS * PEERS and hid % (2 * BF16_ROWS) == 0:
            return grouped(n, *args)
        return gathered(*args)

    in_specs = (
        P(None, "fsdp", None),
        P("section", None),
        P("section", None, None),
        P("section", None, "fsdp", None),
        P("section", None, "fsdp", None),
        P("section", None, "fsdp", None),
        P("section", None, "fsdp", None),
    )
    out_specs = P("section", None, "fsdp", None)
    return jax.shard_map(local, mesh=mesh, in_specs=in_specs, out_specs=out_specs, check_vma=False)
```

```python
import functools

import jax
import jax.numpy as jnp
from jax import lax
from jax.experimental import pallas as pl
from jax.experimental.pallas import tpu as pltpu
from jax.sharding import PartitionSpec as P

MESH = pl.DeviceIdType.MESH
BF16_ROWS = 16
PEERS = 4
AHEAD = 10
LEFT = 4
FIRST = 0
EPS = 1e-05


def silu(v):
    return v / (1.0 + jnp.exp(-v))


def across(lhs, rhs):
    return lax.dot_general(lhs, rhs, (((1,), (1,)), ((), ())), preferred_element_type=jnp.float32)


def plain(lhs, rhs):
    return jnp.dot(lhs, rhs, preferred_element_type=jnp.float32)


def kernel(
    n, most,
    tokens, gain_at, router_at, gate, up, down, ids_at,
    out,
    gain, router, ids, base, held, hnext, early, weights, picked, picked_in, gain_in, outc, outc_in, xbuf, xnext, pbuf, psend, mine, across_part, rest,
    w_send, w_recv, x_send, x_recv, p_send, p_recv, o_send, o_recv, l_sem, go,
):
    sec = lax.axis_index("section")
    me = lax.axis_index("fsdp")
    micros, rows, width = tokens.shape
    hid = gate.shape[0]
    parts = hid // BF16_ROWS
    half = hid // parts
    pieces = most // BF16_ROWS
    group_rows = PEERS * most
    other = 1 - sec

    by_x = 1 - 2 * lax.rem(me, 2)
    by_y = 2 - 4 * lax.rem(lax.div(me, 2), 2)
    by_z = 4 - 8 * lax.rem(lax.div(me, 4), 2)
    by_far = 8 - 16 * lax.rem(lax.div(me, 8), 2)
    near = [me, me + by_z, me + by_far, me + by_z + by_far]
    cross = [me, me + by_y, me + by_z, me + by_y + by_z]
    peer = [a + sec * (b - a) for a, b in zip(near, cross)]
    at_x = me + by_x
    at_y = me + by_y
    far = me + by_far
    inner = lax.rem(lax.div(me, 4) + lax.div(me, 8), 2) == 1
    outer = jnp.logical_not(inner)

    barrier = pltpu.get_barrier_semaphore()
    met = [(sec, p) for p in [at_x, at_y, me + by_z, far, me + by_z + by_far, me + by_y + by_z]] + [(other, p) for p in cross]
    for device in met:
        pl.semaphore_signal(barrier, inc=1, device_id=device, device_id_type=MESH)

    own = (gate, up, down)
    chunks = [(a, h) for a in range(3) for h in range(parts)]

    small = [pltpu.make_async_copy(src, dst, l_sem.at[4 + k]) for k, (src, dst) in enumerate([(ids_at, ids), (gain_at, gain), (router_at, router)])]
    fetch = [pltpu.make_async_copy(tokens, base, l_sem.at[3])]
    fetch += [pltpu.make_async_copy(own[a], weights.at[a, pl.ds(0, hid)], l_sem.at[a]) for a in range(3)]
    for copy in small + fetch[:1]:
        copy.start()

    def weight_copy(slot, chunk, target, send, recv, source_slot=None):
        a, h = chunks[chunk]
        span = pl.ds(h * half, half)
        if source_slot is None:
            src = own[a].at[span]
        else:
            src = weights.at[a, pl.ds(source_slot * hid + h * half, half)]
        return pltpu.make_async_remote_copy(
            src_ref=src,
            dst_ref=weights.at[a, pl.ds(slot * hid + h * half, half)],
            send_sem=w_send.at[send],
            recv_sem=w_recv.at[recv],
            device_id=(sec, target),
            device_id_type=MESH,
        )

    count = len(chunks)
    early_chunks = 2 * parts

    def group(k, chunk):
        return count + 2 * k + (1 if chunk >= early_chunks else 0)

    def x_copy(chunk, single=False):
        return weight_copy(1, chunk, at_x, 0, chunk if single else group(0, chunk))

    def y_copy(chunk, single=False):
        return weight_copy(2, chunk, at_y, 1, chunk if single else group(1, chunk))

    def own_copies(chunk):
        return [x_copy(chunk, chunk % 2 == 1), y_copy(chunk, chunk % 2 == 0)]

    def far_copy(chunk):
        return weight_copy(2, chunk, far, 1, chunk)

    def turn_copy(chunk):
        if chunk % 2 == 0:
            return weight_copy(3, chunk, at_x, 2 if chunk < 2 * LEFT else 4, group(2, chunk), 2)
        return weight_copy(3, chunk, at_y, 3, group(2, chunk), 1)

    def far_turn_copy(chunk):
        return weight_copy(3, chunk, at_x, 2, group(2, chunk), 2)

    def sent(sems, k, ref, some):
        bulk = pltpu.make_async_remote_copy(
            src_ref=ref.at[pl.ds(0, some)], dst_ref=ref.at[pl.ds(0, some)],
            send_sem=sems.at[k], recv_sem=sems.at[k],
            device_id=(other, me), device_id_type=MESH,
        )
        bulk.wait_send()

    def got(sems, k, ref, some):
        bulk = pltpu.make_async_remote_copy(
            src_ref=ref.at[pl.ds(0, some)], dst_ref=ref.at[pl.ds(0, some)],
            send_sem=sems.at[k], recv_sem=sems.at[k],
            device_id=(other, me), device_id_type=MESH,
        )
        bulk.wait_recv()

    def block(m, j):
        return pl.ds((m * PEERS + j) * most, most)

    def share_of(m):
        return pl.ds(m * most, most)

    def token_copy(m, j):
        return pltpu.make_async_remote_copy(
            src_ref=xbuf.at[block(m, 0)], dst_ref=xbuf.at[block(m, j)],
            send_sem=x_send.at[j - 1], recv_sem=x_recv.at[m if j == 2 else micros],
            device_id=(sec, peer[j]), device_id_type=MESH,
        )

    def token_relay(m):
        return pltpu.make_async_remote_copy(
            src_ref=xbuf.at[block(m, PEERS - 2)], dst_ref=xbuf.at[block(m, PEERS - 1)],
            send_sem=x_send.at[0], recv_sem=x_recv.at[micros],
            device_id=(sec, peer[1]), device_id_type=MESH,
        )

    def onward_copy(m, j, q):
        return pltpu.make_async_remote_copy(
            src_ref=xnext.at[pl.ds(m * most + q * BF16_ROWS, BF16_ROWS)], dst_ref=xbuf.at[piece(m, j, q)],
            send_sem=x_send.at[2], recv_sem=x_recv.at[m],
            device_id=(other, cross[j]), device_id_type=MESH,
        )

    def partial_copy(m, j):
        return pltpu.make_async_remote_copy(
            src_ref=psend.at[block(m, j)], dst_ref=pbuf.at[block(m, j)],
            send_sem=p_send.at[0], recv_sem=p_recv.at[m],
            device_id=(sec, peer[j]), device_id_type=MESH,
        )

    def piece(m, j, q):
        return pl.ds((m * PEERS + j) * most + q * BF16_ROWS, BF16_ROWS)

    def inward_copy(m, j, q):
        return pltpu.make_async_remote_copy(
            src_ref=psend.at[piece(m, j, q)], dst_ref=pbuf.at[piece(m, 5 - j, q)],
            send_sem=p_send.at[0], recv_sem=p_recv.at[micros + (m * 2 + 3 - j) * pieces + q],
            device_id=(sec, peer[1]), device_id_type=MESH,
        )

    def share_copy(m, j, q):
        return pltpu.make_async_remote_copy(
            src_ref=psend.at[piece(m, j, q)], dst_ref=pbuf.at[piece(m, j, q)],
            send_sem=p_send.at[0], recv_sem=p_recv.at[m],
            device_id=(sec, peer[j]), device_id_type=MESH,
        )

    def joined_copy(m, j, q):
        return pltpu.make_async_remote_copy(
            src_ref=psend.at[piece(m, j, q)], dst_ref=pbuf.at[piece(m, 0, q)],
            send_sem=p_send.at[0], recv_sem=p_recv.at[m],
            device_id=(sec, peer[j]), device_id_type=MESH,
        )

    def out_copy(m):
        return pltpu.make_async_copy(base.at[m], out.at[m], l_sem.at[m])

    def pass_copy(src, dst, k):
        return pltpu.make_async_remote_copy(
            src_ref=src, dst_ref=dst, send_sem=o_send.at[k], recv_sem=o_recv.at[k],
            device_id=(other, me), device_id_type=MESH,
        )

    pick_copy = pass_copy(picked, picked_in, 0)
    gain_copy = pass_copy(gain, gain_in, 1)
    held_copy = pass_copy(hnext, held, 2)
    outc_copy = pass_copy(outc, outc_in, 3)

    def norm(compact, scale):
        mean_square = jnp.mean(compact * compact, axis=-1, keepdims=True)
        return (compact * lax.rsqrt(mean_square + EPS) * scale).astype(jnp.bfloat16)

    def turned(picks):
        return jnp.transpose(picks.astype(jnp.float32))[0:most].astype(jnp.bfloat16)

    def merge(m, picks, compact, under):
        placed = plain(picks[m][:, 0:most], compact[m * most:(m + 1) * most, :])
        chosen = jnp.sum(picks[m].astype(jnp.float32), axis=1, keepdims=True) > 0.5
        return jnp.where(chosen, placed, under.astype(jnp.float32)).astype(jnp.bfloat16)

    with jax.named_scope("pick"):
        for copy in small:
            copy.wait()
        at_row = lax.broadcasted_iota(jnp.int32, (rows, rows), 0)
        at_col = lax.broadcasted_iota(jnp.int32, (rows, rows), 1)
        lower = jnp.where(at_row >= at_col, 1.0, 0.0).astype(jnp.bfloat16)
        for m in range(micros):
            named = jnp.sum(jnp.where(ids[m] == 0, 1.0, 0.0), axis=0, keepdims=True)
            spread = jnp.transpose(jnp.broadcast_to(named, (rows, rows)))
            rank = plain(lower, spread.astype(jnp.bfloat16))
            hit = (rank.astype(jnp.int32) - 1 == at_col) & (spread > 0.5)
            picked[m] = jnp.where(hit, 1.0, 0.0).astype(jnp.bfloat16)
        fetch[0].wait()
    for copy in fetch[1:]:
        copy.start()

    @pl.when(sec == 0)
    def _():
        for m in range(micros):
            compact = plain(turned(picked[m]), base[m])
            held[share_of(m), :] = compact.astype(jnp.bfloat16)
            xbuf[block(m, 0), :] = norm(compact, gain[...])

    with jax.named_scope("bar"):
        pl.semaphore_wait(barrier, len(met))

    @pl.when(sec == 0)
    def _():
        for m in range(micros):
            for j in range(PEERS - 2, 0, -1):
                token_copy(m, j).start()
        for c in range(len(chunks)):
            for copy in own_copies(c):
                copy.start()
        pick_copy.start()
        pick_copy.wait_recv()
        gain_copy.wait_recv()
        sent(x_send, 1, xbuf, micros * most)
        pl.semaphore_signal(go.at[0], inc=1, device_id=(other, me), device_id_type=MESH)
        for m in range(micros):
            early[share_of(m), :] = plain(turned(picked_in[m]), base[m])

        with jax.named_scope("xrelay"):
            for m in range(micros):
                token_copy(m, PEERS - 2).wait_recv()
                token_relay(m).start()
        for c in range(len(chunks)):
            with jax.named_scope("wrelay"):
                (y_copy if c % 2 == 0 else x_copy)(c, True).wait_recv()
            turn_copy(c).start()
        with jax.named_scope("xsent"):
            sent(w_send, 2, weights.at[0], LEFT * half)
        pl.semaphore_signal(go.at[1], inc=1, device_id=(other, me), device_id_type=MESH)

    @pl.when(sec == 1)
    def _():
        for c in range(FIRST):
            far_copy(c).start()
        gain_copy.start()
        pick_copy.start()
        pick_copy.wait_recv()
        with jax.named_scope("go0"):
            pl.semaphore_wait(go.at[0], 1)
        for c in range(FIRST, AHEAD):
            far_copy(c).start()
        with jax.named_scope("go1"):
            pl.semaphore_wait(go.at[1], 1)
        for c in range(AHEAD):
            x_copy(c).start()
            with jax.named_scope("frelay"):
                far_copy(c).wait_recv()
            far_turn_copy(c).start()
        for c in range(AHEAD, len(chunks)):
            x_copy(c).start()
        with jax.named_scope("go2"):
            pl.semaphore_wait(go.at[2], 1)
        for c in range(AHEAD, len(chunks)):
            far_copy(c).start()
        for c in range(AHEAD, len(chunks)):
            with jax.named_scope("frelay"):
                far_copy(c).wait_recv()
            far_turn_copy(c).start()

    def wait_weights(late, kinds):
        @pl.when(sec == 0)
        def _():
            got(w_recv, count + late, weights.at[0], kinds * hid // 2)
            got(w_recv, count + 2 + late, weights.at[0], kinds * hid // 2)
            got(w_recv, count + 4 + late, weights.at[0], kinds * hid)

        @pl.when(sec == 1)
        def _():
            got(w_recv, count + late, weights.at[0], kinds * hid)
            got(w_recv, count + 4 + late, weights.at[0], kinds * hid)

    for copy in fetch[1:]:
        copy.wait()
    with jax.named_scope("ww"):
        wait_weights(0, 2)

    @pl.when(sec == 0)
    def _():
        with jax.named_scope("wtok"):
            got(x_recv, micros, xbuf, 2 * micros * most)

    for m in range(micros):
        @pl.when(sec == 1)
        def _():
            with jax.named_scope("won"):
                got(x_recv, m, xbuf, PEERS * most)

        with jax.named_scope("gu"):
            x = xbuf[pl.ds(m * group_rows, group_rows), :]
            activated = (silu(across(x, weights[0])) * across(x, weights[1])).astype(jnp.bfloat16)
        if m == 0:
            with jax.named_scope("ww2"):
                wait_weights(1, 1)
        with jax.named_scope("down"):
            partial = plain(activated, weights[2])
            mine[share_of(m), :] = partial[0:most]
            psend[pl.ds(m * group_rows, group_rows), :] = partial.astype(jnp.bfloat16)
        @pl.when(sec == 0)
        def _():
            across_part[pl.ds(m * 2 * most, 2 * most), :] = partial[2 * most:4 * most]

            @pl.when(outer)
            def _():
                for q in range(pieces):
                    for j in (3, 2):
                        inward_copy(m, j, q).start()

            if m == micros - 1:
                for k in range(micros):
                    partial_copy(k, 1).start()

        @pl.when(sec == 1)
        def _():
            for j in range(PEERS - 1, 0, -1):
                for q in range(pieces):
                    share_copy(m, j, q).start()

    @pl.when((sec == 0) & inner)
    def _():
        for m in range(micros):
            for q in range(pieces):
                for j in (2, 3):
                    with jax.named_scope("wearly"):
                        inward_copy(m, 5 - j, q).wait_recv()
                    mine_too = across_part[pl.ds((m * 2 + j - 2) * most + q * BF16_ROWS, BF16_ROWS), :]
                    joined = mine_too + pbuf[piece(m, j, q), :].astype(jnp.float32)
                    psend[piece(m, j, q), :] = joined.astype(jnp.bfloat16)
                    joined_copy(m, j, q).start()
    @pl.when(sec == 1)
    def _():
        held_copy.wait_recv()
        outc_copy.wait_recv()
        for m in range(micros):
            base[m] = merge(m, picked_in, outc_in, base[m])

    for m in range(micros):
        span = share_of(m)
        with jax.named_scope("wpart"):
            score = jnp.sum(xbuf[block(m, 0), :].astype(jnp.float32) * router[...].astype(jnp.float32), axis=1, keepdims=True)
            share = 1.0 / (1.0 + jnp.exp(-score))
            @pl.when(sec == 0)
            def _():
                got(p_recv, m, pbuf, 2 * most)
                if m == 0:
                    pl.semaphore_signal(go.at[2], inc=1, device_id=(other, me), device_id_type=MESH)

            @pl.when(sec == 1)
            def _():
                got(p_recv, m, pbuf, 3 * most)

            update = mine[span, :] + pbuf[block(m, 1), :].astype(jnp.float32)

            @pl.when(sec == 0)
            def _():
                rest[...] = pbuf[block(m, 0), :].astype(jnp.float32)

            @pl.when(sec == 1)
            def _():
                rest[...] = pbuf[block(m, 2), :].astype(jnp.float32) + pbuf[block(m, 3), :].astype(jnp.float32)

            update = update + rest[...]
        outc[span, :] = (held[span, :].astype(jnp.float32) + share * update).astype(jnp.bfloat16)

        @pl.when(sec == 0)
        def _():
            with jax.named_scope("next"):
                again = plain(turned(picked_in[m]), picked[m][:, 0:most])
                changed = jnp.sum(again, axis=1, keepdims=True) > 0.5
                following = jnp.where(changed, plain(again.astype(jnp.bfloat16), outc[span, :]), early[span, :])
                xnext[span, :] = norm(following, gain_in[...])
                hnext[span, :] = following.astype(jnp.bfloat16)
            for j in range(PEERS - 1, -1, -1):
                for q in range(pieces):
                    onward_copy(m, j, q).start()

        @pl.when(sec == 1)
        def _():
            base[m] = merge(m, picked, outc, base[m])
            out_copy(m).start()

    @pl.when(sec == 0)
    def _():
        held_copy.start()
        outc_copy.start()
        for m in range(micros):
            base[m] = merge(m, picked, outc, base[m])
            out_copy(m).start()

    sent(w_send, 0, weights.at[0], 3 * hid)
    sent(w_send, 1, weights.at[0], 3 * hid)
    pick_copy.wait_send()
    for m in range(micros):
        out_copy(m).wait()
    sent(p_send, 0, psend, 3 * micros * most)

    @pl.when(sec == 0)
    def _():
        sent(w_send, 3, weights.at[0], 3 * hid // 2)
        sent(w_send, 4, weights.at[0], (count // 2 - LEFT) * half)
        held_copy.wait_send()
        outc_copy.wait_send()
        sent(x_send, 0, xbuf, 2 * micros * most)
        sent(x_send, 2, xbuf, PEERS * micros * most)

    @pl.when(sec == 1)
    def _():
        sent(w_send, 2, weights.at[0], 3 * hid)
        gain_copy.wait_send()


def grouped(n, tokens, norm_gains, router_cols, gate_weight, up_weight, down_weight, expert_ids):
    micros, rows, width = tokens.shape
    hid = gate_weight.shape[2]
    most = rows // 4
    slots = n // PEERS
    own_rows = micros * most
    chunks = 3 * (hid // BF16_ROWS)
    pieces = most // BF16_ROWS
    all_rows = PEERS * own_rows
    dma = pltpu.SemaphoreType.DMA
    whole = pl.BlockSpec(memory_space=pltpu.HBM)
    half = lambda *shape: pltpu.VMEM(shape, jnp.bfloat16)
    full = lambda *shape: pltpu.VMEM(shape, jnp.float32)
    result = pl.pallas_call(
        functools.partial(kernel, n, most),
        out_shape=jax.ShapeDtypeStruct((micros, rows, width), jnp.bfloat16),
        in_specs=[whole] * 7,
        out_specs=pl.BlockSpec(memory_space=pl.ANY),
        scratch_shapes=[
            full(1, width),
            half(1, width),
            pltpu.VMEM(expert_ids.shape[1:2] + expert_ids.shape[3:1:-1], jnp.int32),
            half(micros, rows, width),
            half(own_rows, width),
            half(own_rows, width),
            full(own_rows, width),
            half(3, slots * hid, width),
            half(micros, rows, rows),
            half(micros, rows, rows),
            full(1, width),
            half(own_rows, width),
            half(own_rows, width),
            half(all_rows, width),
            half(own_rows, width),
            half(all_rows, width),
            half(all_rows, width),
            full(own_rows, width),
            full(2 * own_rows, width),
            full(most, width),
            dma((5,)), dma((chunks + 6,)),
            dma((3,)), dma((micros + 1,)), dma((1,)), dma((micros + 2 * micros * pieces,)),
            dma((4,)), dma((4,)), dma((7,)),
            pltpu.SemaphoreType.REGULAR((3,)),
        ],
        compiler_params=pltpu.CompilerParams(
            collective_id=0, has_side_effects=True, vmem_limit_bytes=24_000_000
        ),
    )(
        *[pltpu.with_memory_space_constraint(a, pltpu.HBM) for a in (
            tokens, norm_gains, router_cols.reshape(1, width),
            gate_weight[0, 0], up_weight[0, 0], down_weight[0, 0], jnp.swapaxes(expert_ids[0], 1, 2),
        )]
    )
    return finish(result)[None]


def finish_kernel(src, dst, sem):
    copies = [pltpu.make_async_copy(src.at[m], dst.at[m], sem.at[m]) for m in range(src.shape[0])]
    for copy in copies:
        copy.start()
    for copy in copies:
        copy.wait()


def finish(result):
    return pl.pallas_call(
        finish_kernel,
        out_shape=jax.ShapeDtypeStruct(result.shape, result.dtype),
        in_specs=[pl.BlockSpec(memory_space=pl.ANY)],
        out_specs=pl.BlockSpec(memory_space=pltpu.HBM),
        scratch_shapes=[pltpu.SemaphoreType.DMA((result.shape[0],))],
        compiler_params=pltpu.CompilerParams(vmem_limit_bytes=4_000_000),
    )(result)


def gathered(tokens, norm_gains, router_cols, gate_weight, up_weight, down_weight, expert_ids):
    section = lax.axis_index("section")
    micros, rows, width = tokens.shape
    stacked = jnp.stack((gate_weight[0, 0], up_weight[0, 0], down_weight[0, 0]))
    panels = lax.all_gather(stacked, "fsdp", axis=1, tiled=True)
    gate, up, down = panels[0], panels[1], panels[2]

    def layer(hidden, routed):
        widened = hidden.astype(jnp.float32)
        mean_square = jnp.mean(widened * widened, axis=-1, keepdims=True)
        normed = (widened * lax.rsqrt(mean_square + EPS) * norm_gains[0]).astype(jnp.bfloat16)
        score = jax.nn.sigmoid(plain(normed, router_cols[0]))[:, 0]
        weight = jnp.where(jnp.any(routed == 0, axis=-1), score, jnp.zeros_like(score))
        activated = (jax.nn.silu(across(normed, gate)) * across(normed, up)).astype(jnp.bfloat16)
        return (widened + weight[:, None] * plain(activated, down)).astype(jnp.bfloat16)

    first = [layer(tokens[m], expert_ids[0, m]) for m in range(micros)]
    coming = [lax.ppermute(f, "section", [(0, 1)]) for f in first]
    second = [layer(coming[m], expert_ids[0, m]) for m in range(micros)]
    return jnp.where(section == 0, jnp.stack(first), jnp.stack(second))[None]


def solution(mesh):
    n = mesh.shape["fsdp"]

    def local(*args):
        hid = args[3].shape[2]
        if n == PEERS * PEERS and hid % (2 * BF16_ROWS) == 0:
            return grouped(n, *args)
        return gathered(*args)

    in_specs = (
        P(None, "fsdp", None),
        P("section", None),
        P("section", None, None),
        P("section", None, "fsdp", None),
        P("section", None, "fsdp", None),
        P("section", None, "fsdp", None),
        P("section", None, "fsdp", None),
    )
    out_specs = P("section", None, "fsdp", None)
    return jax.shard_map(local, mesh=mesh, in_specs=in_specs, out_specs=out_specs, check_vma=False)
```
